512 devices in a mesh: sample: 4 (over y_lo), variant: 32 (over x, z), trait: 4 (over y_hi, core).
Axes of the slice: x: 4, y: 8 (y_hi: 2, y_lo: 4; y = y_hi * 4 + y_lo), z: 8, core: 2. Of those that a mesh axis runs over, the one named last changes fastest.
Arguments:
- dosages: bfloat16 [4096, 65536], P('sample', 'variant')
- phenotypes: float32 [4096, 64], P('sample', 'trait')
- batch_rows: int32 [8, 4096], P(None, 'sample'), may hold values from 0 to 1023
Outputs:
- weights: float32 [64, 65536], P('trait', 'variant')
The draws below stay inside these ranges and needn't reach their ends.
Inputs may be any that keep to these rules, and one draw needn't show every extreme that they name: Draw j of iteration t refers to sample (j // 1024) * 1024 + batch_rows[t-1, j]; draws repeat.
All inputs are finite; a program needn't handle non-finite values.
Results may differ from the reference program's by a relative error of at most 0.0025.
Values may be sent and summed in bfloat16 or wider, within the bound.
A program may use at most 64 MiB of HBM per device.

```python
import math
import jax
import jax.numpy as jnp
from jax import lax

K = 64
S_DEV = 1024
B_DEV = 1024
ITERS = 8
NS = 4096
NV = 65536
MB = 4096


def draw_dosages(key, part):
    key_base, key_scale = jax.random.split(key)
    spread = jnp.exp(jax.random.uniform(key_scale, (1, NV), jnp.float32, math.log(0.3), math.log(3.0)))
    base = jax.random.normal(key_base, (NS, NV), jnp.float32)
    return (base * spread).astype(jnp.bfloat16)


def draw_phenotypes(key, part):
    key_base, key_row = jax.random.split(key, 2)
    row_scale = jnp.exp(jax.random.uniform(key_row, (NS, 1), jnp.float32, math.log(0.3), math.log(3.0)))
    column_scale = 0.3 * jnp.exp(jnp.arange(K, dtype=jnp.float32) / (K - 1) * math.log(10.0))[None, :]
    base = jax.random.normal(key_base, (NS, K), jnp.float32)
    return (base * row_scale * column_scale).astype(jnp.float32)


def place_ends(array, own_key, low, top_value):
    index_at = [jax.random.randint(jax.random.fold_in(own_key, axis), (), 0, length) for axis, length in enumerate(array.shape)]
    widest = array.shape.index(max(array.shape))
    next_to = index_at[:widest] + [(index_at[widest] + 1) % array.shape[widest]] + index_at[widest + 1:]
    return array.at[tuple(index_at)].set(low).at[tuple(next_to)].set(top_value)


def setup_inputs(seed: int = 0) -> dict:
    streams_of = jax.random.split(jax.random.key(seed), 4)
    dosages = draw_dosages(jax.random.fold_in(streams_of[3], 71), 0)
    phenotypes = draw_phenotypes(jax.random.fold_in(streams_of[3], 71), 0)
    batch_rows = place_ends(jax.random.randint(streams_of[2], (ITERS, MB), 0, S_DEV), jax.random.fold_in(streams_of[2], 1), 0, S_DEV - 1).astype(jnp.int32)
    return {"dosages": dosages, "phenotypes": phenotypes, "batch_rows": batch_rows}


def reference(dosages, phenotypes, batch_rows):
    total_rows = dosages.shape[0]
    draws = batch_rows.shape[1]
    offsets = jnp.arange(draws, dtype=jnp.int32) // B_DEV * S_DEV
    pred_scale = 0.06 * math.sqrt(MB) / NV
    grad_scale = 1.0 / math.sqrt(MB)
    weights = jnp.zeros((K, NV), jnp.float32)
    dual = jnp.zeros((K, NV), jnp.float32)
    sample_ids = jnp.arange(total_rows, dtype=jnp.int32)
    for step in range(ITERS):
        turn = step + 1
        picked = batch_rows[step] + offsets
        counts = lax.optimization_barrier(jnp.sum((picked[:, None] == sample_ids[None, :]).astype(jnp.float32), axis=0))
        weights_low = weights.astype(jnp.bfloat16)
        predictions = jnp.dot(dosages, weights_low.T, preferred_element_type=jnp.float32) * pred_scale
        misfit = (counts[:, None] * (predictions - phenotypes)).astype(jnp.bfloat16)
        gradient = jnp.dot(misfit.T, dosages, preferred_element_type=jnp.float32) * grad_scale
        dual = dual + (gradient - dual) / turn
        power = lax.optimization_barrier(jnp.sum(dual * dual, axis=0))
        shrink = jax.nn.relu(1.0 - 20.0 / jnp.sqrt(power + 1e-05))
        weights = -math.sqrt(turn) * shrink[None, :] * dual
    return weights
```

```python
import functools
import math

import jax
import jax.numpy as jnp
from jax import lax
from jax.experimental import pallas as pl
from jax.experimental.pallas import tpu as pltpu
from jax.sharding import PartitionSpec as P

MESH = pl.DeviceIdType.MESH
LANES = 128
NT_DIMS = (((1,), (1,)), ((), ()))


def far_first(n):
    return sorted(range(n), key=lambda o: (-min(o, n - o), o))


def kernel(
    sizes, pred_scale, grad_scale,
    d_ref, ph_ref, rows_ref, out_ref,
    m_buf, gsend, gbuf, wsend, wbuf, psend, pbuf, dual, osend, obuf,
    g_ssem, g_rsem, w_ssem, w_rsem, p_ssem, p_rsem, m_ssem, m_rsem, o_ssem, o_rsem,
):
    ns, nv, nt, iters, nz = sizes
    nx = nv // nz
    chips = ns * nt // 2
    members = chips * 2
    s, v, t = lax.axis_index("sample"), lax.axis_index("variant"), lax.axis_index("trait")
    x, z = v // nz, lax.rem(v, nz)
    core = lax.rem(t, 2)
    y = (t // 2) * ns + s
    me = y * 2 + core

    def member_id(e):
        row = e // 2
        return (lax.rem(row, ns), v, (row // ns) * 2 + lax.rem(e, 2))

    def lanes(i):
        return pl.ds(pl.multiple_of(i * LANES, LANES), LANES)

    def remote(src, dst, ssem, rsem, device):
        return pltpu.make_async_remote_copy(
            src_ref=src, dst_ref=dst, send_sem=ssem, recv_sem=rsem, device_id=device, device_id_type=MESH
        )

    def wait_bytes(ref, sem):
        pltpu.make_async_copy(ref, ref, sem).wait()

    barrier = pltpu.get_barrier_semaphore()

    def greet_column(o, c):
        pl.semaphore_signal(
            barrier, inc=1, device_id=member_id(lax.rem(me + o, members)), device_id_type=MESH
        )
        return c

    def greet_plane(o, c):
        pl.semaphore_signal(barrier, inc=1, device_id=(s, lax.rem(v + o, nv), t), device_id_type=MESH)
        return c

    lax.fori_loop(1, members, greet_column, 0)
    lax.fori_loop(1, nv, greet_plane, 0)

    def counts_of(step, block):
        rows = rows_ref[pl.ds(step, 1), :]
        draws = rows.shape[1]
        ids = lax.broadcasted_iota(jnp.int32, (LANES, draws), 0) + block * LANES
        hot = jnp.where(rows == ids, 1.0, 0.0).astype(jnp.bfloat16)
        ones = jnp.ones((16, draws), jnp.bfloat16)
        return lax.dot_general(ones, hot, NT_DIMS, preferred_element_type=jnp.float32)

    for b in range(nz):
        cols = slice(b * LANES, (b + 1) * LANES)
        m_buf[:, cols] = (counts_of(0, b) * (0.0 - ph_ref[:, cols])).astype(jnp.bfloat16)
    dual[...] = jnp.zeros_like(dual)

    pl.semaphore_wait(barrier, members - 1 + nv - 1)

    def gradient(turn):
        misfit = m_buf[...]
        for o in far_first(chips):
            row = lax.rem(y + o, chips)
            cols = pl.ds(pl.multiple_of(row * 2 * LANES, 2 * LANES), 2 * LANES)
            part = jnp.dot(misfit, d_ref[:, cols], preferred_element_type=jnp.float32) * grad_scale
            for c in range(2):
                gsend[row * 2 + c] = part[:, c * LANES:(c + 1) * LANES]
            for c in range(2):
                e = row * 2 + c
                copy = remote(gsend.at[e], gbuf.at[me], g_ssem, g_rsem, member_id(e))
                if o:
                    copy.start()
                else:
                    pl.when(core != c)(copy.start)
        gbuf[me] = gsend[me]
        wait_bytes(gbuf.at[pl.ds(0, members - 1)], g_rsem)
        power = jnp.zeros((1, LANES), jnp.float32)
        turn_row = jnp.full((1, LANES), turn, jnp.float32)
        for g in range(nt):
            total = None
            for i in range(ns):
                share = gbuf[((g // 2) * ns + i) * 2 + g % 2]
                total = share if total is None else total + share
            old = dual[g]
            new = old + (total - old) / turn_row
            dual[g] = new
            power = power + jnp.sum(new * new, axis=0, keepdims=True)
        wait_bytes(gbuf.at[pl.ds(0, members - 1)], g_ssem)
        shrink = jnp.maximum(1.0 - 20.0 / jnp.sqrt(power + 1e-05), 0.0)
        return -jnp.sqrt(turn_row) * shrink

    def spread(src, dst, ssem, rsem):
        dst[:, lanes(me)] = src[t]

        def send(i, c):
            e = lax.rem(me + members // 2 + i, members)
            pl.when(e != me)(remote(src.at[member_id(e)[2]], dst.at[:, lanes(me)], ssem, rsem, member_id(e)).start)
            return c

        lax.fori_loop(0, members, send, 0)
        rest = dst.at[:, pl.ds(0, (members - 1) * LANES)]
        wait_bytes(rest, rsem)
        wait_bytes(rest, ssem)

    def iteration(turn, carry):
        factor = gradient(turn.astype(jnp.float32))
        for g in range(nt):
            wsend[g] = (factor * dual[g]).astype(jnp.bfloat16)
        spread(wsend, wbuf, w_ssem, w_rsem)

        side = lax.rem(turn, 2)
        weights = wbuf[...]
        pairs = nz // 2
        for o in far_first(pairs):
            pair = lax.rem(z // 2 + o, pairs)
            some = d_ref[pl.ds(pl.multiple_of(pair * 2 * LANES, 2 * LANES), 2 * LANES), :]
            part = lax.dot_general(weights, some, NT_DIMS, preferred_element_type=jnp.float32)
            for c in range(2):
                psend[pair * 2 + c] = part[:, c * LANES:(c + 1) * LANES].astype(jnp.bfloat16)
            for c in range(2):
                for ox in far_first(nx):
                    block = pair * 2 + c
                    to = lax.rem(x + ox, nx) * nz + block
                    copy = remote(psend.at[block], pbuf.at[side, v], p_ssem, p_rsem.at[side], (s, to, t))
                    if o or ox:
                        copy.start()
                    else:
                        pl.when(to != v)(copy.start)
        pbuf[side, v] = psend[z]
        counts = counts_of(turn, z)
        rest = pbuf.at[side, pl.ds(0, nv - 1)]
        wait_bytes(rest, p_rsem.at[side])
        total = jnp.sum(pbuf[side].astype(jnp.float32), axis=0)
        m_buf[:, lanes(z)] = (counts * (total * pred_scale - ph_ref[:, lanes(z)])).astype(jnp.bfloat16)

        def send(o, c):
            to = x * nz + lax.rem(z + o, nz)
            remote(m_buf.at[:, lanes(z)], m_buf.at[:, lanes(z)], m_ssem, m_rsem, (s, to, t)).start()
            return c

        lax.fori_loop(1, nz, send, 0)
        wait_bytes(rest, p_ssem)
        others = m_buf.at[:, pl.ds(0, (nz - 1) * LANES)]
        wait_bytes(others, m_rsem)
        wait_bytes(others, m_ssem)
        return carry

    lax.fori_loop(1, iters, iteration, 0)
    factor = gradient(jnp.float32(iters))
    for g in range(nt):
        osend[g] = factor * dual[g]
    spread(osend, obuf, o_ssem, o_rsem)
    out_ref[...] = obuf[...]


def on_device(sizes, pred_scale, grad_scale, dosages, phenotypes, batch_rows):
    ns, nv, nt, iters, nz = sizes
    samples, width = dosages.shape
    traits = phenotypes.shape[1]
    members = ns * nt
    f32, bf16 = jnp.float32, jnp.bfloat16
    vmem = pl.BlockSpec(memory_space=pltpu.VMEM)
    dma = pltpu.SemaphoreType.DMA
    return pl.pallas_call(
        functools.partial(kernel, sizes, pred_scale, grad_scale),
        out_shape=jax.ShapeDtypeStruct((traits, width), f32),
        in_specs=[vmem] * 3,
        out_specs=vmem,
        scratch_shapes=[
            pltpu.VMEM((traits, samples), bf16),
            pltpu.VMEM((members, traits, LANES), f32),
            pltpu.VMEM((members, traits, LANES), f32),
            pltpu.VMEM((nt, traits, LANES), bf16),
            pltpu.VMEM((traits, width), bf16),
            pltpu.VMEM((nz, traits, LANES), bf16),
            pltpu.VMEM((2, nv, traits, LANES), bf16),
            pltpu.VMEM((nt, traits, LANES), f32),
            pltpu.VMEM((nt, traits, LANES), f32),
            pltpu.VMEM((traits, width), f32),
            dma, dma, dma, dma, dma, dma((2,)), dma, dma, dma, dma,
        ],
        compiler_params=pltpu.CompilerParams(collective_id=0, has_side_effects=True),
        name="dual_averaging",
    )(dosages, phenotypes.T, batch_rows)


def solution(mesh):
    ns, nv, nt = mesh.shape["sample"], mesh.shape["variant"], mesh.shape["trait"]

    def whole(dosages, phenotypes, batch_rows):
        samples, variants = dosages.shape
        draws = batch_rows.shape[1]
        sizes = (ns, nv, nt, batch_rows.shape[0], samples // ns // LANES)
        return jax.shard_map(
            functools.partial(
                on_device, sizes, 0.06 * math.sqrt(draws) / variants, 1.0 / math.sqrt(draws)
            ),
            mesh=mesh,
            in_specs=(P("sample", "variant"), P("sample", "trait"), P(None, "sample")),
            out_specs=P("trait", "variant"),
            check_vma=False,
        )(dosages, phenotypes, batch_rows)

    return whole
```

```python
import functools
import math

import jax
import jax.numpy as jnp
from jax import lax
from jax.experimental import pallas as pl
from jax.experimental.pallas import tpu as pltpu
from jax.sharding import PartitionSpec as P

MESH = pl.DeviceIdType.MESH
WIDE = 256
NT_DIMS = (((1,), (1,)), ((), ()))


def far_first(n):
    return sorted(range(n), key=lambda o: (-min(o, n - o), o))


def near(n):
    return range(-(n // 2), n - n // 2)


def kernel(
    sizes, pred_scale, grad_scale,
    d_hbm, ph_ref, rows_ref, out_ref,
    d_ref, m_buf, gsend, gbuf, wsend, wbuf, psend, pbuf, dual, osend, obuf,
    d_sem, g_ssem, g_rsem, w_ssem, w_rsem, p_ssem, p_rsem, m_ssem, m_rsem, o_ssem, o_rsem,
):
    ns, nv, nt, iters, blocks = sizes
    nz = blocks * 2
    nx = nv // nz
    reps = nt // 2
    chips = ns * reps
    members = chips * 2
    chunks = ns * 2
    half = m_buf.shape[1]
    samples = d_ref.shape[0]
    s, v, t = lax.axis_index("sample"), lax.axis_index("variant"), lax.axis_index("trait")
    x, z = v // nz, lax.rem(v, nz)
    core = lax.rem(t, 2)
    y = (t // 2) * ns + s
    me = y * 2 + core
    chunk = s * 2 + core
    upper, block = lax.rem(x, 2), lax.rem(z, blocks)

    def chip_device(row, c):
        return (lax.rem(row, ns), v, (row // ns) * 2 + c)

    def wide(i):
        return pl.ds(pl.multiple_of(i * WIDE, WIDE), WIDE)

    def remote(src, dst, ssem, rsem, device):
        return pltpu.make_async_remote_copy(
            src_ref=src, dst_ref=dst, send_sem=ssem, recv_sem=rsem, device_id=device, device_id_type=MESH
        )

    def wait_bytes(ref, sem):
        pltpu.make_async_copy(ref, ref, sem).wait()

    barrier = pltpu.get_barrier_semaphore()

    def greet_column(o, c):
        e = lax.rem(me + o, members)
        pl.semaphore_signal(
            barrier, inc=1, device_id=chip_device(e // 2, lax.rem(e, 2)), device_id_type=MESH
        )
        return c

    def greet_plane(o, c):
        pl.semaphore_signal(barrier, inc=1, device_id=(s, lax.rem(v + o, nv), t), device_id_type=MESH)
        return c

    lax.fori_loop(1, nv, greet_plane, 0)
    lax.fori_loop(1, members, greet_column, 0)
    for b in range(blocks):
        rows = pl.ds(b * WIDE, WIDE)
        pltpu.make_async_copy(d_hbm.at[rows], d_ref.at[rows], d_sem).start()

    def counts_of(step, b):
        rows = rows_ref[pl.ds(step, 1), :]
        draws = rows.shape[1]
        ids = lax.broadcasted_iota(jnp.int32, (WIDE, draws), 0) + b * WIDE
        hot = jnp.where(rows == ids, 1.0, 0.0).astype(jnp.bfloat16)
        ones = jnp.ones((2 * half, draws), jnp.bfloat16)
        return lax.dot_general(ones, hot, NT_DIMS, preferred_element_type=jnp.float32)

    for b in range(blocks):
        cols = slice(b * WIDE, (b + 1) * WIDE)
        first = counts_of(0, b) * (0.0 - ph_ref[:, cols])
        for h in range(2):
            m_buf[h, :, cols] = first[h * half:(h + 1) * half].astype(jnp.bfloat16)
    dual[...] = jnp.zeros_like(dual)
    wait_bytes(d_ref, d_sem)
    pl.semaphore_wait(barrier, members - 1 + nv - 1)

    def gradient(turn, side):
        misfit = jnp.concatenate([m_buf[0], m_buf[1]], axis=0)
        for o in far_first(ns)[::-1] if reps > 1 else far_first(ns):
            r = lax.rem(s + o, ns)
            for c in range(2):
                k = r * 2 + c
                part = jnp.dot(misfit, d_ref[:, wide(k)], preferred_element_type=jnp.float32)
                gsend[k] = (part * grad_scale).astype(jnp.bfloat16)
            for rep in range(reps)[::-1]:
                row = lax.rem((y // ns + rep) * ns, chips) + r
                for c in range(2):
                    copy = remote(
                        gsend.at[r * 2 + c], gbuf.at[side, me], g_ssem, g_rsem.at[side], chip_device(row, c)
                    )
                    if o or rep:
                        copy.start()
                    else:
                        pl.when(core != c)(copy.start)
        gbuf[side, me] = gsend[chunk]
        rest = gbuf.at[side, pl.ds(0, members - 1)]
        wait_bytes(rest, g_rsem.at[side])
        power = jnp.zeros((1, WIDE), jnp.float32)
        turn_row = jnp.full((1, WIDE), turn, jnp.float32)
        for g in range(nt):
            total = None
            for i in range(ns):
                share = gbuf[side, ((g // 2) * ns + i) * 2 + g % 2].astype(jnp.float32)
                total = share if total is None else total + share
            old = dual[g]
            fresh = old + (total - old) / turn_row
            dual[g] = fresh
            power = power + jnp.sum(fresh * fresh, axis=0, keepdims=True)
        shrink = jnp.maximum(1.0 - 20.0 / jnp.sqrt(power + 1e-05), 0.0)
        return jnp.sqrt(turn_row) * shrink, rest

    def spread(src, dst, ssem, rsem):
        for o in sorted(near(ns), key=lambda o: -abs(o)):
            row = lax.rem(y + o + chips, chips)
            for c in range(2):
                g = (row // ns) * 2 + c
                copy = remote(src.at[g], dst.at[:, wide(chunk)], ssem, rsem, chip_device(row, c))
                if o:
                    copy.start()
                else:
                    pl.when(core != c)(copy.start)
        dst[:, wide(chunk)] = src[t]
        return dst.at[:, pl.ds(0, (chunks - 1) * WIDE)]

    def iteration(turn, carry):
        side = lax.rem(turn, 2)
        factor, sent = gradient(turn.astype(jnp.float32), side)
        for g in range(nt):
            wsend[g] = (0.0 - factor * dual[g]).astype(jnp.bfloat16)
        rest = spread(wsend, wbuf, w_ssem, w_rsem)
        wait_bytes(sent, g_ssem)
        counts = counts_of(turn, block)[:half]
        wait_bytes(rest, w_rsem)
        wait_bytes(rest, w_ssem)

        weights = wbuf[...]
        for o in far_first(blocks)[::-1]:
            b = lax.rem(block + o, blocks)
            part = lax.dot_general(weights, d_ref[wide(b), :], NT_DIMS, preferred_element_type=jnp.float32)
            for h in range(2):
                psend[b, h] = part[h * half:(h + 1) * half].astype(jnp.bfloat16)
            for oz in sorted((o, o + blocks), key=lambda a: -min(a, nz - a)):
                for ox in far_first(nx):
                    tx = lax.rem(x + ox, nx)
                    to = tx * nz + lax.rem(z + oz, nz)
                    copy = remote(
                        psend.at[b, lax.rem(tx, 2)], pbuf.at[side, v], p_ssem, p_rsem.at[side], (s, to, t)
                    )
                    if ox or oz:
                        copy.start()
        pbuf[side, v] = psend[block, upper]
        rest = pbuf.at[side, pl.ds(0, nv - 1)]
        wait_bytes(rest, p_rsem.at[side])
        total = jnp.sum(pbuf[side].astype(jnp.float32), axis=0)
        traits = pl.ds(pl.multiple_of(upper * half, half), half)
        m_buf[upper, :, wide(block)] = (
            counts * (total * pred_scale - ph_ref[traits, wide(block)])
        ).astype(jnp.bfloat16)
        own = m_buf.at[upper, :, wide(block)]
        for other in (1, 0):
            tx = x + other * (1 - 2 * upper)
            for oz in sorted(near(blocks), key=lambda o: -abs(o)):
                if other or oz:
                    to = tx * nz + lax.rem(z + oz + nz, nz)
                    remote(own, own, m_ssem, m_rsem, (s, to, t)).start()
        wait_bytes(rest, p_ssem)
        for sem in (m_rsem, m_ssem):
            wait_bytes(pbuf.at[1 - side, pl.ds(0, 2 * blocks - 1)], sem)
        return carry

    lax.fori_loop(1, iters, iteration, 0)
    factor, sent = gradient(jnp.float32(iters), iters % 2)
    for g in range(nt):
        osend[g] = factor * dual[g]
    rest = spread(osend, obuf, o_ssem, o_rsem)
    wait_bytes(sent, g_ssem)
    wait_bytes(rest, o_rsem)
    wait_bytes(rest, o_ssem)
    out_ref[...] = obuf[...]


def on_device(sizes, pred_scale, grad_scale, dosages, phenotypes, batch_rows):
    ns, nv, nt, iters, blocks = sizes
    samples, width = dosages.shape
    traits = phenotypes.shape[1]
    members = ns * nt
    half = traits // 2
    f32, bf16 = jnp.float32, jnp.bfloat16
    vmem = pl.BlockSpec(memory_space=pltpu.VMEM)
    dma = pltpu.SemaphoreType.DMA
    negated = pl.pallas_call(
        functools.partial(kernel, sizes, pred_scale, grad_scale),
        out_shape=jax.ShapeDtypeStruct((traits, width), f32),
        in_specs=[pl.BlockSpec(memory_space=pl.ANY), vmem, vmem],
        out_specs=vmem,
        scratch_shapes=[
            pltpu.VMEM((samples, width), bf16),
            pltpu.VMEM((2, half, samples), bf16),
            pltpu.VMEM((ns * 2, traits, WIDE), bf16),
            pltpu.VMEM((2, members, traits, WIDE), bf16),
            pltpu.VMEM((nt, traits, WIDE), bf16),
            pltpu.VMEM((traits, width), bf16),
            pltpu.VMEM((blocks, 2, half, WIDE), bf16),
            pltpu.VMEM((2, nv, half, WIDE), bf16),
            pltpu.VMEM((nt, traits, WIDE), f32),
            pltpu.VMEM((nt, traits, WIDE), f32),
            pltpu.VMEM((traits, width), f32),
            dma, dma, dma((2,)), dma, dma, dma, dma((2,)), dma, dma, dma, dma,
        ],
        compiler_params=pltpu.CompilerParams(collective_id=0, has_side_effects=True),
        name="dual_averaging",
    )(dosages, phenotypes.T, batch_rows)
    return -negated


def solution(mesh):
    ns, nv, nt = mesh.shape["sample"], mesh.shape["variant"], mesh.shape["trait"]

    def whole(dosages, phenotypes, batch_rows):
        samples, variants = dosages.shape
        draws = batch_rows.shape[1]
        sizes = (ns, nv, nt, batch_rows.shape[0], samples // ns // WIDE)
        return jax.shard_map(
            functools.partial(
                on_device, sizes, 0.06 * math.sqrt(draws) / variants, 1.0 / math.sqrt(draws)
            ),
            mesh=mesh,
            in_specs=(P("sample", "variant"), P("sample", "trait"), P(None, "sample")),
            out_specs=P("trait", "variant"),
            check_vma=False,
        )(dosages, phenotypes, batch_rows)

    return whole
```

```python
import functools
import math

import jax
import jax.numpy as jnp
from jax import lax
from jax.experimental import pallas as pl
from jax.experimental.pallas import tpu as pltpu
from jax.sharding import PartitionSpec as P

MESH = pl.DeviceIdType.MESH
WIDE = 256
NT_DIMS = (((1,), (1,)), ((), ()))


def far_first(n):
    return sorted(range(n), key=lambda o: (-min(o, n - o), o))


def near(n, place):
    if n == 1:
        return [0]
    inner = sorted(range(1 - n // 2, n // 2), key=lambda o: -abs(o))
    return [n // 2 * (1 - 2 * (place // (n // 2)))] + inner


def kernel(
    sizes, pred_scale, grad_scale,
    d_hbm, ph_ref, rows_ref, out_ref,
    d_ref, m_buf, gsend, gbuf, wsend, wbuf, psend, pbuf, dual, osend, obuf,
    d_sem, g_ssem, g_rsem, w_ssem, w_rsem, p_ssem, p_rsem, m_ssem, m_rsem, o_ssem, o_rsem,
):
    ns, nv, nt, iters, blocks = sizes
    nz = blocks * 2
    nx = nv // nz
    reps = nt // 2
    chips = ns * reps
    members = chips * 2
    chunks = ns * 2
    half = m_buf.shape[1]
    samples = d_ref.shape[0]
    s, v, t = lax.axis_index("sample"), lax.axis_index("variant"), lax.axis_index("trait")
    x, z = v // nz, lax.rem(v, nz)
    core = lax.rem(t, 2)
    y = (t // 2) * ns + s
    me = y * 2 + core
    chunk = s * 2 + core
    upper, block = lax.rem(x, 2), lax.rem(z, blocks)

    def chip_device(row, c):
        return (lax.rem(row, ns), v, (row // ns) * 2 + c)

    def wide(i):
        return pl.ds(pl.multiple_of(i * WIDE, WIDE), WIDE)

    def remote(src, dst, ssem, rsem, device):
        return pltpu.make_async_remote_copy(
            src_ref=src, dst_ref=dst, send_sem=ssem, recv_sem=rsem, device_id=device, device_id_type=MESH
        )

    def wait_bytes(ref, sem):
        pltpu.make_async_copy(ref, ref, sem).wait()

    barrier = pltpu.get_barrier_semaphore()

    def greet_column(o, c):
        e = lax.rem(me + o, members)
        pl.semaphore_signal(
            barrier, inc=1, device_id=chip_device(e // 2, lax.rem(e, 2)), device_id_type=MESH
        )
        return c

    def greet_plane(o, c):
        pl.semaphore_signal(barrier, inc=1, device_id=(s, lax.rem(v + o, nv), t), device_id_type=MESH)
        return c

    lax.fori_loop(1, nv, greet_plane, 0)
    lax.fori_loop(1, members, greet_column, 0)
    for b in range(blocks):
        rows = pl.ds(b * WIDE, WIDE)
        pltpu.make_async_copy(d_hbm.at[rows], d_ref.at[rows], d_sem).start()

    def counts_of(step, b):
        rows = rows_ref[pl.ds(step, 1), :]
        draws = rows.shape[1]
        ids = lax.broadcasted_iota(jnp.int32, (WIDE, draws), 0) + b * WIDE
        hot = jnp.where(rows == ids, 1.0, 0.0).astype(jnp.bfloat16)
        ones = jnp.ones((2 * half, draws), jnp.bfloat16)
        return lax.dot_general(ones, hot, NT_DIMS, preferred_element_type=jnp.float32)

    for b in range(blocks):
        cols = slice(b * WIDE, (b + 1) * WIDE)
        first = counts_of(0, b) * (0.0 - ph_ref[:, cols])
        for h in range(2):
            m_buf[h, :, cols] = first[h * half:(h + 1) * half].astype(jnp.bfloat16)
    dual[...] = jnp.zeros_like(dual)
    wait_bytes(d_ref, d_sem)
    pl.semaphore_wait(barrier, members - 1 + nv - 1)

    def gradient(turn, side):
        misfit = jnp.concatenate([m_buf[0], m_buf[1]], axis=0)
        for o in far_first(ns)[::-1] if reps > 1 else far_first(ns):
            r = lax.rem(s + o, ns)
            for c in range(2):
                k = r * 2 + c
                part = jnp.dot(misfit, d_ref[:, wide(k)], preferred_element_type=jnp.float32)
                gsend[k] = (part * grad_scale).astype(jnp.bfloat16)
            for rep in range(reps)[::-1]:
                row = lax.rem((y // ns + rep) * ns, chips) + r
                for c in range(2):
                    copy = remote(
                        gsend.at[r * 2 + c], gbuf.at[side, me], g_ssem, g_rsem.at[side], chip_device(row, c)
                    )
                    if o or rep:
                        copy.start()
                    else:
                        pl.when(core != c)(copy.start)
        gbuf[side, me] = gsend[chunk]
        rest = gbuf.at[side, pl.ds(0, members - 1)]
        wait_bytes(rest, g_rsem.at[side])
        power = jnp.zeros((1, WIDE), jnp.float32)
        turn_row = jnp.full((1, WIDE), turn, jnp.float32)
        for g in range(nt):
            total = None
            for i in range(ns):
                share = gbuf[side, ((g // 2) * ns + i) * 2 + g % 2].astype(jnp.float32)
                total = share if total is None else total + share
            old = dual[g]
            fresh = old + (total - old) / turn_row
            dual[g] = fresh
            power = power + jnp.sum(fresh * fresh, axis=0, keepdims=True)
        shrink = jnp.maximum(1.0 - 20.0 / jnp.sqrt(power + 1e-05), 0.0)
        return jnp.sqrt(turn_row) * shrink, rest

    def spread(src, dst, ssem, rsem):
        for i, o in enumerate(near(ns, s)):
            row = lax.rem(y + o + chips, chips)
            for c in range(2):
                g = (row // ns) * 2 + c
                copy = remote(src.at[g], dst.at[:, wide(chunk)], ssem, rsem, chip_device(row, c))
                if i < ns - 1:
                    copy.start()
                else:
                    pl.when(core != c)(copy.start)
        dst[:, wide(chunk)] = src[t]
        return dst.at[:, pl.ds(0, (chunks - 1) * WIDE)]

    def iteration(turn, carry):
        side = lax.rem(turn, 2)
        factor, sent = gradient(turn.astype(jnp.float32), side)
        for g in range(nt):
            wsend[g] = (0.0 - factor * dual[g]).astype(jnp.bfloat16)
        rest = spread(wsend, wbuf, w_ssem, w_rsem)
        wait_bytes(sent, g_ssem)
        counts = counts_of(turn, block)[:half]
        wait_bytes(rest, w_rsem)
        wait_bytes(rest, w_ssem)

        weights = wbuf[...]
        for o in far_first(blocks)[::-1]:
            b = lax.rem(block + o, blocks)
            part = lax.dot_general(weights, d_ref[wide(b), :], NT_DIMS, preferred_element_type=jnp.float32)
            for h in range(2):
                psend[b, h] = part[h * half:(h + 1) * half].astype(jnp.bfloat16)
            for oz in sorted((o, o + blocks), key=lambda a: -min(a, nz - a)):
                for ox in far_first(nx):
                    tx = lax.rem(x + ox, nx)
                    to = tx * nz + lax.rem(z + oz, nz)
                    copy = remote(
                        psend.at[b, lax.rem(tx, 2)], pbuf.at[side, v], p_ssem, p_rsem.at[side], (s, to, t)
                    )
                    if ox or oz:
                        copy.start()
        pbuf[side, v] = psend[block, upper]
        rest = pbuf.at[side, pl.ds(0, nv - 1)]
        wait_bytes(rest, p_rsem.at[side])
        total = jnp.sum(pbuf[side].astype(jnp.float32), axis=0)
        traits = pl.ds(pl.multiple_of(upper * half, half), half)
        m_buf[upper, :, wide(block)] = (
            counts * (total * pred_scale - ph_ref[traits, wide(block)])
        ).astype(jnp.bfloat16)
        own = m_buf.at[upper, :, wide(block)]
        for other in (1, 0):
            tx = x + other * (1 - 2 * upper)
            for i, oz in enumerate(near(blocks, block)):
                if other or i < blocks - 1:
                    to = tx * nz + lax.rem(z + oz + nz, nz)
                    remote(own, own, m_ssem, m_rsem, (s, to, t)).start()
        wait_bytes(rest, p_ssem)
        for sem in (m_rsem, m_ssem):
            wait_bytes(pbuf.at[1 - side, pl.ds(0, 2 * blocks - 1)], sem)
        return carry

    lax.fori_loop(1, iters, iteration, 0)
    factor, sent = gradient(jnp.float32(iters), iters % 2)
    for g in range(nt):
        osend[g] = factor * dual[g]
    rest = spread(osend, obuf, o_ssem, o_rsem)
    wait_bytes(sent, g_ssem)
    wait_bytes(rest, o_rsem)
    wait_bytes(rest, o_ssem)
    out_ref[...] = obuf[...]


def on_device(sizes, pred_scale, grad_scale, dosages, phenotypes, batch_rows):
    ns, nv, nt, iters, blocks = sizes
    samples, width = dosages.shape
    traits = phenotypes.shape[1]
    members = ns * nt
    half = traits // 2
    f32, bf16 = jnp.float32, jnp.bfloat16
    vmem = pl.BlockSpec(memory_space=pltpu.VMEM)
    dma = pltpu.SemaphoreType.DMA
    negated = pl.pallas_call(
        functools.partial(kernel, sizes, pred_scale, grad_scale),
        out_shape=jax.ShapeDtypeStruct((traits, width), f32),
        in_specs=[pl.BlockSpec(memory_space=pl.ANY), vmem, vmem],
        out_specs=vmem,
        scratch_shapes=[
            pltpu.VMEM((samples, width), bf16),
            pltpu.VMEM((2, half, samples), bf16),
            pltpu.VMEM((ns * 2, traits, WIDE), bf16),
            pltpu.VMEM((2, members, traits, WIDE), bf16),
            pltpu.VMEM((nt, traits, WIDE), bf16),
            pltpu.VMEM((traits, width), bf16),
            pltpu.VMEM((blocks, 2, half, WIDE), bf16),
            pltpu.VMEM((2, nv, half, WIDE), bf16),
            pltpu.VMEM((nt, traits, WIDE), f32),
            pltpu.VMEM((nt, traits, WIDE), f32),
            pltpu.VMEM((traits, width), f32),
            dma, dma, dma((2,)), dma, dma, dma, dma((2,)), dma, dma, dma, dma,
        ],
        compiler_params=pltpu.CompilerParams(collective_id=0, has_side_effects=True),
        name="dual_averaging",
    )(dosages, phenotypes.T, batch_rows)
    return -negated


def solution(mesh):
    ns, nv, nt = mesh.shape["sample"], mesh.shape["variant"], mesh.shape["trait"]

    def whole(dosages, phenotypes, batch_rows):
        samples, variants = dosages.shape
        draws = batch_rows.shape[1]
        sizes = (ns, nv, nt, batch_rows.shape[0], samples // ns // WIDE)
        return jax.shard_map(
            functools.partial(
                on_device, sizes, 0.06 * math.sqrt(draws) / variants, 1.0 / math.sqrt(draws)
            ),
            mesh=mesh,
            in_specs=(P("sample", "variant"), P("sample", "trait"), P(None, "sample")),
            out_specs=P("trait", "variant"),
            check_vma=False,
        )(dosages, phenotypes, batch_rows)

    return whole
```

```python
import functools
import math

import jax
import jax.numpy as jnp
from jax import lax
from jax.experimental import pallas as pl
from jax.experimental.pallas import tpu as pltpu
from jax.sharding import PartitionSpec as P

MESH = pl.DeviceIdType.MESH
WIDE = 256
NT_DIMS = (((1,), (1,)), ((), ()))


def far_first(n):
    return sorted(range(n), key=lambda o: (-min(o, n - o), o))


def near(n, place):
    if n == 1:
        return [0]
    inner = sorted(range(1 - n // 2, n // 2), key=lambda o: -abs(o))
    return [n // 2 * (1 - 2 * (place // (n // 2)))] + inner


def kernel(
    sizes, pred_scale, grad_scale,
    d_hbm, ph_ref, rows_ref, out_ref,
    d_ref, m_buf, gsend, gbuf, wsend, wbuf, psend, pbuf, dual, osend, obuf,
    d_sem, g_ssem, g_rsem, w_ssem, w_rsem, p_ssem, p_rsem, m_ssem, m_rsem, o_ssem, o_rsem,
):
    ns, nv, nt, iters, blocks = sizes
    nz = blocks * 2
    nx = nv // nz
    reps = nt // 2
    chips = ns * reps
    members = chips * 2
    chunks = ns * 2
    half = m_buf.shape[1]
    samples = d_ref.shape[0]
    s, v, t = lax.axis_index("sample"), lax.axis_index("variant"), lax.axis_index("trait")
    x, z = v // nz, lax.rem(v, nz)
    core = lax.rem(t, 2)
    y = (t // 2) * ns + s
    me = y * 2 + core
    chunk = s * 2 + core
    upper, block = lax.rem(x, 2), lax.rem(z, blocks)

    def chip_device(row, c):
        return (lax.rem(row, ns), v, (row // ns) * 2 + c)

    def wide(i):
        return pl.ds(pl.multiple_of(i * WIDE, WIDE), WIDE)

    def remote(src, dst, ssem, rsem, device):
        return pltpu.make_async_remote_copy(
            src_ref=src, dst_ref=dst, send_sem=ssem, recv_sem=rsem, device_id=device, device_id_type=MESH
        )

    def wait_bytes(ref, sem):
        pltpu.make_async_copy(ref, ref, sem).wait()

    barrier = pltpu.get_barrier_semaphore()

    def greet_column(o, c):
        e = lax.rem(me + o, members)
        pl.semaphore_signal(
            barrier, inc=1, device_id=chip_device(e // 2, lax.rem(e, 2)), device_id_type=MESH
        )
        return c

    def greet_plane(o, c):
        pl.semaphore_signal(barrier, inc=1, device_id=(s, lax.rem(v + o, nv), t), device_id_type=MESH)
        return c

    lax.fori_loop(1, nv, greet_plane, 0)
    lax.fori_loop(1, members, greet_column, 0)
    for b in range(blocks):
        rows = pl.ds(b * WIDE, WIDE)
        pltpu.make_async_copy(d_hbm.at[rows], d_ref.at[rows], d_sem).start()

    def counts_of(step, b):
        rows = rows_ref[pl.ds(step, 1), :]
        draws = rows.shape[1]
        ids = lax.broadcasted_iota(jnp.int32, (WIDE, draws), 0) + b * WIDE
        hot = jnp.where(rows == ids, 1.0, 0.0).astype(jnp.bfloat16)
        ones = jnp.ones((2 * half, draws), jnp.bfloat16)
        return lax.dot_general(ones, hot, NT_DIMS, preferred_element_type=jnp.float32)

    for b in range(blocks):
        cols = slice(b * WIDE, (b + 1) * WIDE)
        first = counts_of(0, b) * (0.0 - ph_ref[:, cols])
        for h in range(2):
            m_buf[h, :, cols] = first[h * half:(h + 1) * half].astype(jnp.bfloat16)
    dual[...] = jnp.zeros_like(dual)
    wait_bytes(d_ref, d_sem)
    pl.semaphore_wait(barrier, members - 1 + nv - 1)

    def gradient(turn, side):
        misfit = jnp.concatenate([m_buf[0], m_buf[1]], axis=0)
        for o in far_first(ns)[::-1] if reps > 1 else far_first(ns):
            r = lax.rem(s + o, ns)
            for c in range(2):
                k = r * 2 + c
                part = jnp.dot(misfit, d_ref[:, wide(k)], preferred_element_type=jnp.float32)
                gsend[k] = (part * grad_scale).astype(jnp.bfloat16)
            for rep in range(reps)[::-1]:
                row = lax.rem((y // ns + rep) * ns, chips) + r
                for c in range(2):
                    copy = remote(
                        gsend.at[r * 2 + c], gbuf.at[side, me], g_ssem, g_rsem.at[side], chip_device(row, c)
                    )
                    if o or rep:
                        copy.start()
                    else:
                        pl.when(core != c)(copy.start)
        gbuf[side, me] = gsend[chunk]
        rest = gbuf.at[side, pl.ds(0, members - 1)]
        wait_bytes(rest, g_rsem.at[side])
        power = jnp.zeros((1, WIDE), jnp.float32)
        turn_row = jnp.full((1, WIDE), turn, jnp.float32)
        for g in range(nt):
            total = None
            for i in range(ns):
                share = gbuf[side, ((g // 2) * ns + i) * 2 + g % 2].astype(jnp.float32)
                total = share if total is None else total + share
            old = dual[g]
            fresh = old + (total - old) / turn_row
            dual[g] = fresh
            power = power + jnp.sum(fresh * fresh, axis=0, keepdims=True)
        shrink = jnp.maximum(1.0 - 20.0 / jnp.sqrt(power + 1e-05), 0.0)
        return jnp.sqrt(turn_row) * shrink

    def spread(src, dst, ssem, rsem):
        for i, o in enumerate(near(ns, s)):
            row = lax.rem(y + o + chips, chips)
            for c in range(2):
                g = (row // ns) * 2 + c
                copy = remote(src.at[g], dst.at[:, wide(chunk)], ssem, rsem, chip_device(row, c))
                if i < ns - 1:
                    copy.start()
                else:
                    pl.when(core != c)(copy.start)
        dst[:, wide(chunk)] = src[t]
        return dst.at[:, pl.ds(0, (chunks - 1) * WIDE)]

    g_sent = gbuf.at[0, pl.ds(0, members - 1)]
    p_sent = pbuf.at[0, pl.ds(0, nv - 1)]
    m_sent = pbuf.at[0, pl.ds(0, 2 * blocks - 1)]

    def iteration(turn, factor):
        side = lax.rem(turn, 2)
        for g in range(nt):
            wsend[g] = (0.0 - factor * dual[g]).astype(jnp.bfloat16)
        w_sent = spread(wsend, wbuf, w_ssem, w_rsem)
        counts = counts_of(turn, block)[:half]
        wait_bytes(w_sent, w_rsem)

        weights = wbuf[...]
        for o in far_first(blocks)[::-1]:
            b = lax.rem(block + o, blocks)
            part = lax.dot_general(weights, d_ref[wide(b), :], NT_DIMS, preferred_element_type=jnp.float32)
            for h in range(2):
                psend[b, h] = part[h * half:(h + 1) * half].astype(jnp.bfloat16)
            for oz in sorted((o, o + blocks), key=lambda a: -min(a, nz - a)):
                for ox in far_first(nx):
                    tx = lax.rem(x + ox, nx)
                    to = tx * nz + lax.rem(z + oz, nz)
                    copy = remote(
                        psend.at[b, lax.rem(tx, 2)], pbuf.at[side, v], p_ssem, p_rsem.at[side], (s, to, t)
                    )
                    if ox or oz:
                        copy.start()
        pbuf[side, v] = psend[block, upper]
        rest = pbuf.at[side, pl.ds(0, nv - 1)]
        wait_bytes(rest, p_rsem.at[side])
        total = jnp.sum(pbuf[side].astype(jnp.float32), axis=0)
        traits = pl.ds(pl.multiple_of(upper * half, half), half)
        m_buf[upper, :, wide(block)] = (
            counts * (total * pred_scale - ph_ref[traits, wide(block)])
        ).astype(jnp.bfloat16)
        own = m_buf.at[upper, :, wide(block)]
        for other in (1, 0):
            tx = x + other * (1 - 2 * upper)
            for i, oz in enumerate(near(blocks, block)):
                if other or i < blocks - 1:
                    to = tx * nz + lax.rem(z + oz + nz, nz)
                    remote(own, own, m_ssem, m_rsem, (s, to, t)).start()
        wait_bytes(g_sent, g_ssem)
        wait_bytes(w_sent, w_ssem)
        wait_bytes(m_sent, m_rsem)
        factor = gradient((turn + 1).astype(jnp.float32), 1 - side)
        wait_bytes(p_sent, p_ssem)
        wait_bytes(m_sent, m_ssem)
        return factor

    factor = lax.fori_loop(1, iters, iteration, gradient(jnp.float32(1), 1))
    for g in range(nt):
        osend[g] = factor * dual[g]
    rest = spread(osend, obuf, o_ssem, o_rsem)
    wait_bytes(g_sent, g_ssem)
    wait_bytes(rest, o_rsem)
    wait_bytes(rest, o_ssem)
    out_ref[...] = obuf[...]


def on_device(sizes, pred_scale, grad_scale, dosages, phenotypes, batch_rows):
    ns, nv, nt, iters, blocks = sizes
    samples, width = dosages.shape
    traits = phenotypes.shape[1]
    members = ns * nt
    half = traits // 2
    f32, bf16 = jnp.float32, jnp.bfloat16
    vmem = pl.BlockSpec(memory_space=pltpu.VMEM)
    dma = pltpu.SemaphoreType.DMA
    negated = pl.pallas_call(
        functools.partial(kernel, sizes, pred_scale, grad_scale),
        out_shape=jax.ShapeDtypeStruct((traits, width), f32),
        in_specs=[pl.BlockSpec(memory_space=pl.ANY), vmem, vmem],
        out_specs=vmem,
        scratch_shapes=[
            pltpu.VMEM((samples, width), bf16),
            pltpu.VMEM((2, half, samples), bf16),
            pltpu.VMEM((ns * 2, traits, WIDE), bf16),
            pltpu.VMEM((2, members, traits, WIDE), bf16),
            pltpu.VMEM((nt, traits, WIDE), bf16),
            pltpu.VMEM((traits, width), bf16),
            pltpu.VMEM((blocks, 2, half, WIDE), bf16),
            pltpu.VMEM((2, nv, half, WIDE), bf16),
            pltpu.VMEM((nt, traits, WIDE), f32),
            pltpu.VMEM((nt, traits, WIDE), f32),
            pltpu.VMEM((traits, width), f32),
            dma, dma, dma((2,)), dma, dma, dma, dma((2,)), dma, dma, dma, dma,
        ],
        compiler_params=pltpu.CompilerParams(collective_id=0, has_side_effects=True),
        name="dual_averaging",
    )(dosages, phenotypes.T, batch_rows)
    return -negated


def solution(mesh):
    ns, nv, nt = mesh.shape["sample"], mesh.shape["variant"], mesh.shape["trait"]

    def whole(dosages, phenotypes, batch_rows):
        samples, variants = dosages.shape
        draws = batch_rows.shape[1]
        sizes = (ns, nv, nt, batch_rows.shape[0], samples // ns // WIDE)
        return jax.shard_map(
            functools.partial(
                on_device, sizes, 0.06 * math.sqrt(draws) / variants, 1.0 / math.sqrt(draws)
            ),
            mesh=mesh,
            in_specs=(P("sample", "variant"), P("sample", "trait"), P(None, "sample")),
            out_specs=P("trait", "variant"),
            check_vma=False,
        )(dosages, phenotypes, batch_rows)

    return whole
```

```python
import functools
import math

import jax
import jax.numpy as jnp
from jax import lax
from jax.experimental import pallas as pl
from jax.experimental.pallas import tpu as pltpu
from jax.sharding import PartitionSpec as P

MESH = pl.DeviceIdType.MESH
WIDE = 256
NT_DIMS = (((1,), (1,)), ((), ()))


def far_first(n):
    return sorted(range(n), key=lambda o: (-min(o, n - o), o))


def near(n, place):
    if n == 1:
        return [0]
    inner = sorted(range(1 - n // 2, n // 2), key=lambda o: -abs(o))
    return [n // 2 * (1 - 2 * (place // (n // 2)))] + inner


def kernel(
    sizes, pred_scale, grad_scale,
    d_hbm, ph_ref, rows_ref, out_ref,
    d_ref, m_buf, gsend, gbuf, wsend, wbuf, psend, pbuf, dual, osend, obuf,
    d_sem, g_ssem, g_rsem, w_ssem, w_rsem, p_ssem, p_rsem, m_ssem, m_rsem, o_ssem, o_rsem,
):
    ns, nv, nt, iters, blocks = sizes
    nz = blocks * 2
    nx = nv // nz
    reps = nt // 2
    chips = ns * reps
    members = chips * 2
    chunks = ns * 2
    half = m_buf.shape[1]
    samples = d_ref.shape[0]
    s, v, t = lax.axis_index("sample"), lax.axis_index("variant"), lax.axis_index("trait")
    x, z = v // nz, lax.rem(v, nz)
    core = lax.rem(t, 2)
    y = (t // 2) * ns + s
    me = y * 2 + core
    chunk = s * 2 + core
    upper, block = lax.rem(x, 2), lax.rem(z, blocks)

    def chip_device(row, c):
        return (lax.rem(row, ns), v, (row // ns) * 2 + c)

    def wide(i):
        return pl.ds(pl.multiple_of(i * WIDE, WIDE), WIDE)

    def remote(src, dst, ssem, rsem, device):
        return pltpu.make_async_remote_copy(
            src_ref=src, dst_ref=dst, send_sem=ssem, recv_sem=rsem, device_id=device, device_id_type=MESH
        )

    def wait_bytes(ref, sem):
        pltpu.make_async_copy(ref, ref, sem).wait()

    barrier = pltpu.get_barrier_semaphore()

    def far(o, n):
        return lax.rem(o - 1 + n // 2, n - 1) + 1

    def greet_column(o, c):
        e = lax.rem(me + far(o, members), members)
        pl.semaphore_signal(
            barrier, inc=1, device_id=chip_device(e // 2, lax.rem(e, 2)), device_id_type=MESH
        )
        return c

    def greet_plane(o, c):
        pl.semaphore_signal(barrier, inc=1, device_id=(s, lax.rem(v + far(o, nv), nv), t), device_id_type=MESH)
        return c

    lax.fori_loop(1, nv, greet_plane, 0)
    lax.fori_loop(1, members, greet_column, 0)
    for b in range(blocks):
        rows = pl.ds(b * WIDE, WIDE)
        pltpu.make_async_copy(d_hbm.at[rows], d_ref.at[rows], d_sem).start()

    def counts_of(step, b):
        rows = rows_ref[pl.ds(step, 1), :]
        draws = rows.shape[1]
        ids = lax.broadcasted_iota(jnp.int32, (WIDE, draws), 0) + b * WIDE
        hot = jnp.where(rows == ids, 1.0, 0.0).astype(jnp.bfloat16)
        ones = jnp.ones((2 * half, draws), jnp.bfloat16)
        return lax.dot_general(ones, hot, NT_DIMS, preferred_element_type=jnp.float32)

    for b in range(blocks):
        cols = slice(b * WIDE, (b + 1) * WIDE)
        first = counts_of(0, b) * (0.0 - ph_ref[:, cols])
        for h in range(2):
            m_buf[h, :, cols] = first[h * half:(h + 1) * half].astype(jnp.bfloat16)
    dual[...] = jnp.zeros_like(dual)
    wait_bytes(d_ref, d_sem)
    pl.semaphore_wait(barrier, members - 1 + nv - 1)

    def gradient(turn, side):
        misfit = jnp.concatenate([m_buf[0], m_buf[1]], axis=0)
        for o in far_first(ns)[::-1] if reps > 1 else far_first(ns):
            r = lax.rem(s + o, ns)
            for c in range(2):
                k = r * 2 + c
                part = jnp.dot(misfit, d_ref[:, wide(k)], preferred_element_type=jnp.float32)
                gsend[k] = (part * grad_scale).astype(jnp.bfloat16)
                for rep in range(reps)[::-1]:
                    row = lax.rem((y // ns + rep) * ns, chips) + r
                    copy = remote(
                        gsend.at[k], gbuf.at[side, me], g_ssem, g_rsem.at[side], chip_device(row, c)
                    )
                    if o or rep:
                        copy.start()
                    else:
                        pl.when(core != c)(copy.start)
        gbuf[side, me] = gsend[chunk]
        rest = gbuf.at[side, pl.ds(0, members - 1)]
        wait_bytes(rest, g_rsem.at[side])
        power = jnp.zeros((1, WIDE), jnp.float32)
        turn_row = jnp.full((1, WIDE), turn, jnp.float32)
        for g in range(nt):
            total = None
            for i in range(ns):
                share = gbuf[side, ((g // 2) * ns + i) * 2 + g % 2].astype(jnp.float32)
                total = share if total is None else total + share
            old = dual[g]
            fresh = old + (total - old) / turn_row
            dual[g] = fresh
            power = power + jnp.sum(fresh * fresh, axis=0, keepdims=True)
        shrink = jnp.maximum(1.0 - 20.0 / jnp.sqrt(power + 1e-05), 0.0)
        return jnp.sqrt(turn_row) * shrink, rest

    def spread(src, dst, ssem, rsem):
        for i, o in enumerate(near(ns, s)):
            row = lax.rem(y + o + chips, chips)
            for c in range(2):
                g = (row // ns) * 2 + c
                copy = remote(src.at[g], dst.at[:, wide(chunk)], ssem, rsem, chip_device(row, c))
                if i < ns - 1:
                    copy.start()
                else:
                    pl.when(core != c)(copy.start)
        dst[:, wide(chunk)] = src[t]
        return dst.at[:, pl.ds(0, (chunks - 1) * WIDE)]

    def iteration(turn, carry):
        side = lax.rem(turn, 2)
        factor, sent = gradient(turn.astype(jnp.float32), side)
        for g in range(nt):
            wsend[g] = (0.0 - factor * dual[g]).astype(jnp.bfloat16)
        rest = spread(wsend, wbuf, w_ssem, w_rsem)
        wait_bytes(sent, g_ssem)
        counts = counts_of(turn, block)[:half]
        wait_bytes(rest, w_rsem)
        wait_bytes(rest, w_ssem)

        weights = wbuf[...]
        for o in far_first(blocks)[::-1]:
            b = lax.rem(block + o, blocks)
            part = lax.dot_general(weights, d_ref[wide(b), :], NT_DIMS, preferred_element_type=jnp.float32)
            for h in range(2):
                psend[b, h] = part[h * half:(h + 1) * half].astype(jnp.bfloat16)
            for oz in sorted((o, o + blocks), key=lambda a: -min(a, nz - a)):
                for ox in far_first(nx):
                    tx = lax.rem(x + ox, nx)
                    to = tx * nz + lax.rem(z + oz, nz)
                    copy = remote(
                        psend.at[b, lax.rem(tx, 2)], pbuf.at[side, v], p_ssem, p_rsem.at[side], (s, to, t)
                    )
                    if ox or oz:
                        copy.start()
        pbuf[side, v] = psend[block, upper]
        rest = pbuf.at[side, pl.ds(0, nv - 1)]
        wait_bytes(rest, p_rsem.at[side])
        total = jnp.sum(pbuf[side].astype(jnp.float32), axis=0)
        traits = pl.ds(pl.multiple_of(upper * half, half), half)
        m_buf[upper, :, wide(block)] = (
            counts * (total * pred_scale - ph_ref[traits, wide(block)])
        ).astype(jnp.bfloat16)
        own = m_buf.at[upper, :, wide(block)]
        for other in (1, 0):
            tx = x + other * (1 - 2 * upper)
            for i, oz in enumerate(near(blocks, block)):
                if other or i < blocks - 1:
                    to = tx * nz + lax.rem(z + oz + nz, nz)
                    remote(own, own, m_ssem, m_rsem, (s, to, t)).start()
        wait_bytes(rest, p_ssem)
        for sem in (m_rsem, m_ssem):
            wait_bytes(pbuf.at[1 - side, pl.ds(0, 2 * blocks - 1)], sem)
        return carry

    lax.fori_loop(1, iters, iteration, 0)
    factor, sent = gradient(jnp.float32(iters), iters % 2)
    for g in range(nt):
        osend[g] = factor * dual[g]
    rest = spread(osend, obuf, o_ssem, o_rsem)
    wait_bytes(sent, g_ssem)
    wait_bytes(rest, o_rsem)
    wait_bytes(rest, o_ssem)
    out_ref[...] = obuf[...]


def on_device(sizes, pred_scale, grad_scale, dosages, phenotypes, batch_rows):
    ns, nv, nt, iters, blocks = sizes
    samples, width = dosages.shape
    traits = phenotypes.shape[1]
    members = ns * nt
    half = traits // 2
    f32, bf16 = jnp.float32, jnp.bfloat16
    vmem = pl.BlockSpec(memory_space=pltpu.VMEM)
    dma = pltpu.SemaphoreType.DMA
    negated = pl.pallas_call(
        functools.partial(kernel, sizes, pred_scale, grad_scale),
        out_shape=jax.ShapeDtypeStruct((traits, width), f32),
        in_specs=[pl.BlockSpec(memory_space=pl.ANY), vmem, vmem],
        out_specs=vmem,
        scratch_shapes=[
            pltpu.VMEM((samples, width), bf16),
            pltpu.VMEM((2, half, samples), bf16),
            pltpu.VMEM((ns * 2, traits, WIDE), bf16),
            pltpu.VMEM((2, members, traits, WIDE), bf16),
            pltpu.VMEM((nt, traits, WIDE), bf16),
            pltpu.VMEM((traits, width), bf16),
            pltpu.VMEM((blocks, 2, half, WIDE), bf16),
            pltpu.VMEM((2, nv, half, WIDE), bf16),
            pltpu.VMEM((nt, traits, WIDE), f32),
            pltpu.VMEM((nt, traits, WIDE), f32),
            pltpu.VMEM((traits, width), f32),
            dma, dma, dma((2,)), dma, dma, dma, dma((2,)), dma, dma, dma, dma,
        ],
        compiler_params=pltpu.CompilerParams(collective_id=0, has_side_effects=True),
        name="dual_averaging",
    )(dosages, phenotypes.T, batch_rows)
    return -negated


def solution(mesh):
    ns, nv, nt = mesh.shape["sample"], mesh.shape["variant"], mesh.shape["trait"]

    def whole(dosages, phenotypes, batch_rows):
        samples, variants = dosages.shape
        draws = batch_rows.shape[1]
        sizes = (ns, nv, nt, batch_rows.shape[0], samples // ns // WIDE)
        return jax.shard_map(
            functools.partial(
                on_device, sizes, 0.06 * math.sqrt(draws) / variants, 1.0 / math.sqrt(draws)
            ),
            mesh=mesh,
            in_specs=(P("sample", "variant"), P("sample", "trait"), P(None, "sample")),
            out_specs=P("trait", "variant"),
            check_vma=False,
        )(dosages, phenotypes, batch_rows)

    return whole
```
